32 devices in a mesh: cuts: 4 (over z), blk: 2 (over x), rep: 4 (over y, core).
Axes of the slice: x: 2, y: 2, z: 4, core: 2. Of those that a mesh axis runs over, the one named last changes fastest.
Arguments:
- features: bfloat16 [8192, 256], P(('cuts', 'blk', 'rep')), may hold values from -6 to 6
- adj_values: bfloat16 [64, 4, 128, 1024], P(('cuts', 'blk'), 'rep'), as said below
- adj_cols: int32 [64, 4, 8], P(('cuts', 'blk'), 'rep'), may hold values from 0 to 15, as said below
- adj_count: int32 [64, 4], P(('cuts', 'blk'), 'rep'), may hold values from 1 to 8, as said below
- weight: bfloat16 [256, 256], replicated, may hold values from -0.375 to 0.375
- cotangent: bfloat16 [8192, 256], P(('cuts', 'blk', 'rep')), may hold values from -6 to 6
Outputs:
- output: bfloat16 [8192, 256], P(('cuts', 'blk', 'rep'))
- weight_grad: float32 [256, 256], replicated
The draws below stay inside these ranges and needn't reach their ends.
Inputs may be any that keep to these rules, and one draw needn't show every extreme that they name: `adj_values`: entries are nonnegative; a row of a block has about 8 nonzero entries on average. `adj_cols`: within one row block and rep index the 8 numbers are distinct. `adj_count`: in every aligned group of 8 row blocks, for every rep index, some row block has count 8.
All inputs are finite; a program needn't handle non-finite values.
Results may differ from the reference program's by a relative error of at most 0.0061.
Values may be sent and summed in bfloat16 or wider, within the bound.
A program may use at most 64 MiB of HBM per device.

```python
import jax
import jax.numpy as jnp
from jax import lax

BS = 128
F = 256
NB_DEV = 2
EDGES_ROW = 8
COLS = 16
SLOTS = 8
GROUP_BLK = 8
ROWBLOCKS = 64
NODES = 8192
N_REP = 4


def draw_adj_values(key, part):
    first, second = jax.random.split(jax.random.fold_in(key, 11))
    shape = (ROWBLOCKS, N_REP, BS, SLOTS * BS)
    keep = jax.random.uniform(first, shape, jnp.float32) < EDGES_ROW / BS
    magnitude = jax.random.uniform(second, shape, jnp.float32, 0.5, 1.5)
    scale = (EDGES_ROW * SLOTS * N_REP / 2.0) ** (-0.5)
    values = jnp.where(keep, magnitude * scale, jnp.zeros((), jnp.float32))
    return values.astype(jnp.bfloat16)


def draw_adj_cols(key, part):
    keys = jax.random.split(key, ROWBLOCKS * N_REP)

    def one_list(single):
        return jax.random.permutation(single, COLS)[:SLOTS]
    columns = jax.vmap(one_list)(keys)
    return columns.reshape(ROWBLOCKS, N_REP, SLOTS).astype(jnp.int32)


def draw_adj_count(key, part):
    first, second = jax.random.split(key)
    base = jax.random.randint(first, (ROWBLOCKS, N_REP), 1, SLOTS + 1)
    groups = ROWBLOCKS // GROUP_BLK
    chosen = jax.random.randint(second, (groups, 1, N_REP), 0, GROUP_BLK)
    position = jnp.arange(GROUP_BLK, dtype=jnp.int32)[None, :, None]
    filled = (position == chosen).reshape(ROWBLOCKS, N_REP)
    return jnp.where(filled, SLOTS, base).astype(jnp.int32)


def spiked(array, stream_key, source, target, shards_of, factor):
    owner, partner = [(jnp.arange(array.shape[dim]) // (array.shape[dim] // shards_of)).reshape([-1 if axis == dim else 1 for axis in range(array.ndim)]) for dim in (source, target)]
    chosen = jax.random.permutation(stream_key, shards_of)[partner]
    strong = (owner == chosen) | (owner == (partner + shards_of // 2) % shards_of)
    return jnp.where(strong, factor * array, array)


def shard_levels(key, dims, shards, smallest, top_value):
    loudness = 1.0
    for dim, shards_of in shards:
        steps = jax.random.uniform(jax.random.fold_in(jax.random.fold_in(key, 6), dim), (shards_of,), jnp.float32, smallest / len(shards), top_value / len(shards))
        loudness = loudness * jnp.repeat(jnp.exp(steps), dims[dim] // shards_of).reshape((-1,) + (1,) * (len(dims) - 1 - dim))
    return loudness


def bell_draw(key, dims, width, most, shards=(), kind=jnp.bfloat16):
    values = jax.random.normal(key, dims, jnp.float32) * width
    if len(shards) > 0:
        values = shard_levels(key, dims, shards, -0.22, 0.18) * values
    return jnp.clip(values, min=-most, max=most).astype(kind)


def gaussian_with(own_key, extent, scale, bound, shards, heavy, held_as=jnp.bfloat16):
    entries = scale * jax.random.normal(own_key, extent, jnp.float32)
    if shards:
        entries = entries * shard_levels(own_key, extent, shards, -0.22, 0.18)
    return jnp.clip(spiked(entries, jax.random.fold_in(own_key, 3), *heavy), -bound, bound).astype(held_as)


def setup_inputs(seed: int = 0) -> dict:
    streams_of = jax.random.split(jax.random.key(seed), 7)
    features = bell_draw(streams_of[0], (NODES, F), 1.0, 6.0, ((0, 32),))
    adj_values = draw_adj_values(jax.random.fold_in(streams_of[6], 71), 0)
    adj_cols = draw_adj_cols(jax.random.fold_in(streams_of[6], 71), 0)
    adj_count = draw_adj_count(jax.random.fold_in(streams_of[6], 71), 0)
    weight = bell_draw(streams_of[4], (F, F), F ** -0.5, 0.375)
    cotangent = gaussian_with(streams_of[5], (NODES, F), 1.0, 6.0, ((0, 32),), (0, 1, 32, 2.75))
    return {"features": features, "adj_values": adj_values, "adj_cols": adj_cols, "adj_count": adj_count, "weight": weight, "cotangent": cotangent}


def silu_grad(pre):
    sigmoid_z = jax.nn.sigmoid(pre)
    return sigmoid_z * (1.0 + pre * (1.0 - sigmoid_z))

def reference(features, adj_values, adj_cols, adj_count, weight, cotangent):
    panel_blocks = features.reshape(ROWBLOCKS, BS, F)
    rep_ids = jnp.arange(N_REP, dtype=jnp.int32)[:, None]
    slot_ids = jnp.arange(SLOTS, dtype=jnp.int32)[None, :]

    def row_block(packed):
        block_values, columns, counts = packed
        global_ids = (columns // NB_DEV * N_REP + rep_ids) * NB_DEV + columns % NB_DEV
        picked = panel_blocks[global_ids].astype(jnp.float32)
        usable = slot_ids < counts[:, None]
        picked = jnp.where(usable[:, :, None, None], picked, jnp.zeros((), jnp.float32))
        dense = block_values.astype(jnp.float32).reshape(N_REP, BS, SLOTS, BS)
        return jnp.einsum('rask,rskf->af', dense, picked)
    summed = lax.map(row_block, (adj_values, adj_cols, adj_count))
    hidden = summed.reshape(NODES, F).astype(jnp.bfloat16)
    pre = jnp.dot(hidden, weight, preferred_element_type=jnp.float32)
    output = jax.nn.silu(pre).astype(jnp.bfloat16)
    grad_pre = (cotangent.astype(jnp.float32) * silu_grad(pre)).astype(jnp.bfloat16)
    weight_grad = lax.dot_general(hidden, grad_pre, (((0,), (0,)), ((), ())), preferred_element_type=jnp.float32)
    return (output, weight_grad)
```

```python
import functools

import jax
import jax.numpy as jnp
from jax import lax
from jax.experimental import pallas as pl
from jax.experimental.pallas import tpu as pltpu
from jax.sharding import PartitionSpec as P

MESH = pl.DeviceIdType.MESH
BF = jnp.bfloat16
F32 = jnp.float32


def silu_grad(pre):
    sigmoid_z = jax.nn.sigmoid(pre)
    return sigmoid_z * (1.0 + pre * (1.0 - sigmoid_z))


def local(features, adj_values, adj_cols, adj_count, weight, cotangent):
    block_size = adj_values.shape[2]
    slot_count = adj_cols.shape[2]
    feature_width = features.shape[1]
    group_rows = adj_values.shape[0]
    in_slice = lax.all_gather(features, "blk", axis=0, tiled=True)
    gathered = lax.all_gather(in_slice, "cuts", axis=0, tiled=True)
    panel_blocks = gathered.reshape(-1, block_size, feature_width)
    columns = adj_cols[:, 0, :]
    picked = panel_blocks[columns]
    slot_ids = jnp.arange(slot_count, dtype=jnp.int32)[None, :]
    usable = slot_ids < adj_count[:, 0][:, None]
    picked = jnp.where(usable[:, :, None, None], picked, jnp.zeros((), jnp.bfloat16))
    picked = picked.reshape(group_rows, slot_count * block_size, feature_width)
    partial_value = lax.dot_general(
        adj_values[:, 0], picked, (((2,), (1,)), ((0,), (0,))), preferred_element_type=jnp.float32
    )
    partial_value = partial_value.reshape(group_rows * block_size, feature_width)
    summed = lax.psum_scatter(partial_value, "rep", scatter_dimension=0, tiled=True)
    hidden = summed.astype(jnp.bfloat16)
    pre = jnp.dot(hidden, weight, preferred_element_type=jnp.float32)
    output = jax.nn.silu(pre).astype(jnp.bfloat16)
    grad_pre = (cotangent.astype(jnp.float32) * silu_grad(pre)).astype(jnp.bfloat16)
    local_grad = lax.dot_general(
        hidden, grad_pre, (((0,), (0,)), ((), ())), preferred_element_type=jnp.float32
    )
    weight_grad = lax.psum(local_grad, ("cuts", "blk", "rep"))
    return (output, weight_grad)


def fused_kernel(
    nz, rows, slots, bs,
    feat_ref, adj_ref, cols_ref, count_ref, w_ref, cot_ref,
    out_ref, wg_ref,
    panel, adjv, dense, acc, wv, cotv, b1s, b1r, b2s, b2r, hid, stage, parts, gath,
    local_sem, adj_sem, a_send, a_recv, b_send, b_recv, d_send, d_recv,
):
    z = lax.axis_index("cuts")
    x = lax.axis_index("blk")
    r = lax.axis_index("rep")
    nx, nrep = 2, 4
    ndev = nz * nx * nrep
    me = (z * nx + x) * nrep + r
    own = z * nx + x

    def coords(p):
        return (p // (nx * nrep), (p // nrep) % nx, p % nrep)

    barrier = pltpu.get_barrier_semaphore()

    def greet(k, carry):
        pl.semaphore_signal(
            barrier, inc=1, device_id=coords((me + k) % ndev), device_id_type=MESH
        )
        return carry

    lax.fori_loop(1, ndev, greet, 0)
    own_copy = pltpu.make_async_copy(feat_ref, panel.at[own], local_sem.at[0])
    own_copy.start()
    adj_copies = [
        pltpu.make_async_copy(
            adj_ref.at[:, 0, :, pl.ds(k * bs, bs)], adjv.at[k], adj_sem.at[k]
        )
        for k in range(slots)
    ]
    for copy in adj_copies:
        copy.start()
    w_copy = pltpu.make_async_copy(w_ref, wv, local_sem.at[1])
    w_copy.start()
    cot_copy = pltpu.make_async_copy(cot_ref, cotv, local_sem.at[2])
    cot_copy.start()
    own_copy.wait()
    pl.semaphore_wait(barrier, ndev - 1)

    def hop(direction, src_z, src_x, c):
        target = ((z + 1, x, r), (z - 1, x, r), (z, 1 - x, r))[direction]
        piece = panel.at[src_z * nx + src_x, pl.ds(c * bs, bs)]
        return pltpu.make_async_remote_copy(
            src_ref=piece,
            dst_ref=piece,
            send_sem=a_send.at[direction, src_z, c],
            recv_sem=a_recv.at[src_z * nx + src_x, c],
            device_id=target,
            device_id_type=MESH,
        )

    def arrive(src_z, src_x, c):
        hop(2, src_z, src_x, c).wait_recv()

    for c in range(2):
        @pl.when(z < nz - 1)
        def _():
            hop(0, z, x, c).start()

        @pl.when(z > 0)
        def _():
            hop(1, z, x, c).start()

        hop(2, z, x, c).start()

    for copy in adj_copies:
        copy.wait()

    def spread(t, carry):
        i = t // nz // nx
        s = t % (nz * nx)
        count = count_ref[i]
        for c in range(2):
            q = s * 2 + c
            slot = jnp.int32(0)
            used = jnp.int32(0)
            for k in range(slots):
                hit = jnp.where((cols_ref[i, 0, k] == q) & (k < count), 1, 0)
                slot = slot + hit * k
                used = used + hit
            block = adjv[slot, i]
            scale = used.astype(F32).astype(BF)
            dense[s, pl.ds(pl.multiple_of(i * bs, bs), bs), c * bs:(c + 1) * bs] = block * scale
        return carry

    lax.fori_loop(0, rows * nz * nx, spread, 0)

    def multiply(s, first=False):
        def tile(t, carry):
            a = dense[s, pl.ds(pl.multiple_of(t * 2 * bs, 2 * bs), 2 * bs), :]
            product = jnp.dot(a, panel[s], preferred_element_type=F32)
            if first:
                acc[t] = product
            else:
                acc[t] = acc[t] + product
            return carry

        lax.fori_loop(0, nrep, tile, 0)

    multiply(own, first=True)
    for d in range(1, nz + 1):
        for c in range(2):
            @pl.when(z - d >= 0)
            def _():
                arrive(z - d, x, c)

                @pl.when(z < nz - 1)
                def _():
                    hop(0, z - d, x, c).start()

                hop(2, z - d, x, c).start()

            @pl.when(z + d < nz)
            def _():
                arrive(z + d, x, c)

                @pl.when(z > 0)
                def _():
                    hop(1, z + d, x, c).start()

                hop(2, z + d, x, c).start()

        @pl.when(z - d >= 0)
        def _():
            multiply((z - d) * nx + x)

        @pl.when(z + d < nz)
        def _():
            multiply((z + d) * nx + x)

        for src_z in ((z,) if d == 1 else (z - d + 1, z + d - 1)):
            @pl.when((src_z >= 0) & (src_z < nz))
            def _():
                for c in range(2):
                    arrive(src_z, 1 - x, c)
                multiply(src_z * nx + 1 - x)

    y = r // 2
    core = r % 2
    mate = y * 2 + 1 - core
    cross = (1 - y) * 2 + core
    far = (1 - y) * 2 + 1 - core

    def to_mate(k):
        return pltpu.make_async_remote_copy(
            src_ref=b1s.at[k], dst_ref=b1r.at[k],
            send_sem=b_send.at[k], recv_sem=b_recv.at[k],
            device_id=(z, x, mate), device_id_type=MESH,
        )

    def to_cross(c):
        piece = pl.ds(c * bs, bs)
        return pltpu.make_async_remote_copy(
            src_ref=b2s.at[piece], dst_ref=b2r.at[piece],
            send_sem=b_send.at[2 + c], recv_sem=b_recv.at[2 + c],
            device_id=(z, x, cross), device_id_type=MESH,
        )

    b1s[0] = acc[far].astype(BF)
    to_mate(0).start()
    b1s[1] = acc[mate].astype(BF)
    to_mate(1).start()
    to_mate(0).wait_recv()
    for c in range(2):
        piece = slice(c * bs, (c + 1) * bs)
        b2s[piece] = (acc[cross, piece] + b1r[0, piece].astype(F32)).astype(BF)
        to_cross(c).start()
    to_mate(1).wait_recv()
    w_copy.wait()
    cot_copy.wait()
    for c in range(2):
        piece = slice(c * bs, (c + 1) * bs)
        known = acc[r, piece] + b1r[1, piece].astype(F32)
        to_cross(c).wait_recv()
        hid[piece] = (known + b2r[piece].astype(F32)).astype(BF)
    hidden = hid[...]
    pre = jnp.dot(hidden, wv[...], preferred_element_type=F32)
    sigmoid_z = 1.0 / (1.0 + jnp.exp(-pre))
    grad_pre = (
        cotv[...].astype(F32) * (sigmoid_z * (1.0 + pre * (1.0 - sigmoid_z)))
    ).astype(BF)
    grad = lax.dot_general(
        hidden, grad_pre, (((0,), (0,)), ((), ())), preferred_element_type=F32
    ).astype(BF)
    tall = 16
    for p in range(ndev):
        stage[p] = grad[p // 2 * tall:(p // 2 + 1) * tall, p % 2 * 128:(p % 2 + 1) * 128]

    def scatter(k):
        p = (me + k) % ndev
        return pltpu.make_async_remote_copy(
            src_ref=stage.at[p], dst_ref=parts.at[k],
            send_sem=d_send.at[0], recv_sem=d_recv.at[0],
            device_id=coords(p), device_id_type=MESH,
        )

    def spray(k):
        p = (me + k) % ndev
        return pltpu.make_async_remote_copy(
            src_ref=gath.at[me], dst_ref=gath.at[me],
            send_sem=d_send.at[1], recv_sem=d_recv.at[1],
            device_id=coords(p), device_id_type=MESH,
        )

    def everyone(send):
        def one(k, carry):
            send(k).start()
            return carry

        lax.fori_loop(1, ndev, one, 0)

    def all_of(buf, k):
        whole = buf.at[pl.ds(1, ndev - 1)]
        return pltpu.make_async_remote_copy(
            src_ref=whole, dst_ref=whole,
            send_sem=d_send.at[k], recv_sem=d_recv.at[k],
            device_id=(z, x, mate), device_id_type=MESH,
        )

    everyone(scatter)
    out_ref[...] = (pre * sigmoid_z).astype(BF)
    total = stage[me].astype(F32)
    all_of(parts, 0).wait_recv()
    for k in range(1, ndev):
        total = total + parts[k].astype(F32)
    gath[me] = total.astype(BF)
    everyone(spray)

    for k in range(2):
        to_mate(k).wait_send()
        to_cross(k).wait_send()
    for c in range(2):
        for src in range(nz):
            @pl.when((z < nz - 1) & (src <= z))
            def _():
                hop(0, src, x, c).wait_send()

            @pl.when((z > 0) & (src >= z))
            def _():
                hop(1, src, x, c).wait_send()

            hop(2, src, x, c).wait_send()
    all_of(stage, 0).wait_send()
    all_of(gath, 1).wait_recv()
    for p in range(ndev):
        wg_ref[p // 2 * tall:(p // 2 + 1) * tall, p % 2 * 128:(p % 2 + 1) * 128] = gath[p].astype(F32)
    all_of(gath, 1).wait_send()


def fused(nz, features, adj_values, adj_cols, adj_count, weight, cotangent):
    rows, _, bs, wide = adj_values.shape
    slots = wide // bs
    width = features.shape[1]
    ndev = nz * 8
    hbm = pl.BlockSpec(memory_space=pl.ANY)
    smem = pl.BlockSpec(memory_space=pltpu.SMEM)
    vmem = pl.BlockSpec(memory_space=pltpu.VMEM)
    own = features.shape[0]
    return pl.pallas_call(
        functools.partial(fused_kernel, nz, rows, slots, bs),
        out_shape=(
            jax.ShapeDtypeStruct(features.shape, BF),
            jax.ShapeDtypeStruct(weight.shape, F32),
        ),
        in_specs=[hbm, hbm, smem, smem, hbm, hbm],
        out_specs=(vmem, vmem),
        scratch_shapes=[
            pltpu.VMEM((nz * 2, own, width), BF),
            pltpu.VMEM((slots, rows, bs, bs), BF),
            pltpu.VMEM((nz * 2, rows * bs, own), BF),
            pltpu.VMEM((4, own, width), F32),
            pltpu.VMEM(weight.shape, BF),
            pltpu.VMEM((own, width), BF),
            pltpu.VMEM((2, own, width), BF),
            pltpu.VMEM((2, own, width), BF),
            pltpu.VMEM((own, width), BF),
            pltpu.VMEM((own, width), BF),
            pltpu.VMEM((own, width), BF),
            pltpu.VMEM((ndev, 16, 128), BF),
            pltpu.VMEM((ndev, 16, 128), BF),
            pltpu.VMEM((ndev, 16, 128), BF),
            pltpu.SemaphoreType.DMA((3,)),
            pltpu.SemaphoreType.DMA((slots,)),
            pltpu.SemaphoreType.DMA((3, nz, 2)),
            pltpu.SemaphoreType.DMA((nz * 2, 2)),
            pltpu.SemaphoreType.DMA((4,)),
            pltpu.SemaphoreType.DMA((4,)),
            pltpu.SemaphoreType.DMA((2,)),
            pltpu.SemaphoreType.DMA((2,)),
        ],
        compiler_params=pltpu.CompilerParams(collective_id=0, has_side_effects=True),
    )(features, adj_values, adj_cols, adj_count.reshape(-1), weight, cotangent)


def solution(mesh):
    placed = (
        P(("cuts", "blk", "rep"), None),
        P(("cuts", "blk"), "rep", None, None),
        P(("cuts", "blk"), "rep", None),
        P(("cuts", "blk"), "rep"),
        P(),
        P(("cuts", "blk", "rep"), None),
    )
    sizes = (mesh.shape["cuts"], mesh.shape["blk"], mesh.shape["rep"])
    body = functools.partial(fused, sizes[0]) if sizes == (4, 2, 4) else local
    return jax.shard_map(
        body,
        mesh=mesh,
        in_specs=placed,
        out_specs=(P(("cuts", "blk", "rep"), None), P()),
        check_vma=False,
    )
```

```python
import functools

import jax
import jax.numpy as jnp
from jax import lax
from jax.experimental import pallas as pl
from jax.experimental.pallas import tpu as pltpu
from jax.sharding import PartitionSpec as P

MESH = pl.DeviceIdType.MESH
BF = jnp.bfloat16
F32 = jnp.float32


def silu_grad(pre):
    sigmoid_z = jax.nn.sigmoid(pre)
    return sigmoid_z * (1.0 + pre * (1.0 - sigmoid_z))


def local(features, adj_values, adj_cols, adj_count, weight, cotangent):
    block_size = adj_values.shape[2]
    slot_count = adj_cols.shape[2]
    feature_width = features.shape[1]
    group_rows = adj_values.shape[0]
    in_slice = lax.all_gather(features, "blk", axis=0, tiled=True)
    gathered = lax.all_gather(in_slice, "cuts", axis=0, tiled=True)
    panel_blocks = gathered.reshape(-1, block_size, feature_width)
    columns = adj_cols[:, 0, :]
    picked = panel_blocks[columns]
    slot_ids = jnp.arange(slot_count, dtype=jnp.int32)[None, :]
    usable = slot_ids < adj_count[:, 0][:, None]
    picked = jnp.where(usable[:, :, None, None], picked, jnp.zeros((), jnp.bfloat16))
    picked = picked.reshape(group_rows, slot_count * block_size, feature_width)
    partial_value = lax.dot_general(
        adj_values[:, 0], picked, (((2,), (1,)), ((0,), (0,))), preferred_element_type=jnp.float32
    )
    partial_value = partial_value.reshape(group_rows * block_size, feature_width)
    summed = lax.psum_scatter(partial_value, "rep", scatter_dimension=0, tiled=True)
    hidden = summed.astype(jnp.bfloat16)
    pre = jnp.dot(hidden, weight, preferred_element_type=jnp.float32)
    output = jax.nn.silu(pre).astype(jnp.bfloat16)
    grad_pre = (cotangent.astype(jnp.float32) * silu_grad(pre)).astype(jnp.bfloat16)
    local_grad = lax.dot_general(
        hidden, grad_pre, (((0,), (0,)), ((), ())), preferred_element_type=jnp.float32
    )
    weight_grad = lax.psum(local_grad, ("cuts", "blk", "rep"))
    return (output, weight_grad)


def fused_kernel(
    nz, rows, slots, bs,
    feat_ref, adj_ref, cols_ref, count_ref, w_ref, cot_ref,
    out_ref, sum_ref,
    panel, adjv, dense, acc, wv, cotv, b1s, b1r, b2s, b2r, hid, outv, stage, parts, gath,
    local_sem, adj_sem, a_send, a_recv, b_send, b_recv, d_send, d_recv,
):
    z = lax.axis_index("cuts")
    x = lax.axis_index("blk")
    r = lax.axis_index("rep")
    nx, nrep = 2, 4
    ndev = nz * nx * nrep
    me = (z * nx + x) * nrep + r
    own = z * nx + x

    def coords(p):
        return (p // (nx * nrep), (p // nrep) % nx, p % nrep)

    y = r // 2
    core = r % 2
    mate = y * 2 + 1 - core
    cross = (1 - y) * 2 + core
    far = (1 - y) * 2 + 1 - core

    barrier = pltpu.get_barrier_semaphore()

    def greet(device):
        pl.semaphore_signal(barrier, inc=1, device_id=device, device_id_type=MESH)

    @pl.when(z < nz - 1)
    def _():
        greet((z + 1, x, r))

    @pl.when(z > 0)
    def _():
        greet((z - 1, x, r))

    greet((z, 1 - x, r))
    greet((z, x, mate))
    greet((z, x, cross))
    own_copy = pltpu.make_async_copy(feat_ref, panel.at[own], local_sem.at[0])
    own_copy.start()
    adj_copies = [
        pltpu.make_async_copy(
            adj_ref.at[:, 0, :, pl.ds(k * bs, bs)], adjv.at[k], adj_sem.at[k]
        )
        for k in range(slots)
    ]
    for copy in adj_copies:
        copy.start()
    w_copy = pltpu.make_async_copy(w_ref, wv, local_sem.at[1])
    w_copy.start()
    cot_copy = pltpu.make_async_copy(cot_ref, cotv, local_sem.at[2])
    cot_copy.start()
    own_copy.wait()
    @pl.when((z > 0) & (z < nz - 1))
    def _():
        pl.semaphore_wait(barrier, 5)

    @pl.when((z == 0) | (z == nz - 1))
    def _():
        pl.semaphore_wait(barrier, 4)

    pieces = 4
    step = 2 * bs // pieces

    def hop(direction, src_z, src_x, c):
        target = ((z + 1, x, r), (z - 1, x, r), (z, 1 - x, r))[direction]
        piece = panel.at[src_z * nx + src_x, pl.ds(c * step, step)]
        return pltpu.make_async_remote_copy(
            src_ref=piece,
            dst_ref=piece,
            send_sem=a_send.at[direction, src_z * nx + src_x, c],
            recv_sem=a_recv.at[src_z * nx + src_x, c],
            device_id=target,
            device_id_type=MESH,
        )

    def arrive(src_z, src_x, c):
        hop(2, src_z, src_x, c).wait_recv()

    for c, across in zip(range(pieces), (2, 3, 0, 1)):
        @pl.when(z < nz - 1)
        def _():
            hop(0, z, x, c).start()

        @pl.when(z > 0)
        def _():
            hop(1, z, x, c).start()

        hop(2, z, x, across).start()

    for copy in adj_copies:
        copy.wait()

    def spread(src_z, src_x):
        s = src_z * nx + src_x

        def one(i, carry):
            count = count_ref[i]
            for c in range(2):
                q = s * 2 + c
                slot = jnp.int32(0)
                used = jnp.int32(0)
                for k in range(slots):
                    hit = jnp.where((cols_ref[i, 0, k] == q) & (k < count), 1, 0)
                    slot = slot + hit * k
                    used = used + hit
                block = adjv[slot, i]
                scale = used.astype(F32).astype(BF)
                dense[s, pl.ds(pl.multiple_of(i * bs, bs), bs), c * bs:(c + 1) * bs] = block * scale
            return carry

        lax.fori_loop(0, rows, one, 0, unroll=2)

    order = (
        (z, x), (z, 1 - x),
        ((z + 1) % nz, x), ((z + nz - 1) % nz, x),
        ((z + 1) % nz, 1 - x), ((z + nz - 1) % nz, 1 - x),
        ((z + 2) % nz, x), ((z + 2) % nz, 1 - x),
    )
    def multiply(s, first=False):
        def tile(t, carry):
            a = dense[s, pl.ds(pl.multiple_of(t * 2 * bs, 2 * bs), 2 * bs), :]
            product = jnp.dot(a, panel[s], preferred_element_type=F32)
            if first:
                acc[t] = product
            else:
                acc[t] = acc[t] + product
            return carry

        lax.fori_loop(0, nrep, tile, 0)

    spread(*order[0])
    spread(*order[1])
    for d in range(1, nz):
        for c in range(pieces):
            late = False

            @pl.when(z - d >= 0)
            def _():
                arrive(z - d, x, c)

                @pl.when(z < nz - 1)
                def _():
                    hop(0, z - d, x, c).start()

                if late:
                    @pl.when(z - d > 0)
                    def _():
                        hop(2, z - d, x, c).start()
                else:
                    hop(2, z - d, x, c).start()

            @pl.when(z + d < nz)
            def _():
                arrive(z + d, x, c)

                @pl.when(z > 0)
                def _():
                    hop(1, z + d, x, c).start()

                if late:
                    @pl.when(z + d < nz - 1)
                    def _():
                        hop(2, z + d, x, c).start()
                else:
                    hop(2, z + d, x, c).start()

            if False:
                @pl.when(z + d - 1 == nz - 1)
                def _():
                    arrive(nz - 1, 1 - x, c + pieces // 2)
                    hop(1, nz - 1, 1 - x, c + pieces // 2).start()

                @pl.when(z - (d - 1) == 0)
                def _():
                    arrive(0, 1 - x, c + pieces // 2)
                    hop(0, 0, 1 - x, c + pieces // 2).start()

            if d == 1:
                if c < 2:
                    spread(*order[2 + c])
                elif c == 2:
                    multiply(own, first=True)
            elif d == 2:
                spread(*order[4 + c])

        @pl.when(z - d >= 0)
        def _():
            multiply((z - d) * nx + x)

        @pl.when(z + d < nz)
        def _():
            multiply((z + d) * nx + x)

        near = d - 1
        for src_z in ((z,) if d == 1 else (z - near, z + near)):
            @pl.when((src_z >= 0) & (src_z < nz))
            def _():
                for c in range(pieces):
                    if False:
                        passed = (src_z == nz - 1) | (src_z == 0)

                        @pl.when(jnp.logical_not(passed))
                        def _():
                            arrive(src_z, 1 - x, c)
                    else:
                        arrive(src_z, 1 - x, c)
                multiply(src_z * nx + 1 - x)

    for src_z in (z - (nz - 1), z + nz - 1):
        @pl.when((src_z >= 0) & (src_z < nz))
        def _():
            for c in range(pieces):
                arrive(src_z, 1 - x, c)
            multiply(src_z * nx + 1 - x)

    def to_mate(k):
        return pltpu.make_async_remote_copy(
            src_ref=b1s.at[k], dst_ref=b1r.at[k],
            send_sem=b_send.at[k], recv_sem=b_recv.at[k],
            device_id=(z, x, mate), device_id_type=MESH,
        )

    def to_cross(c):
        piece = pl.ds(c * bs, bs)
        return pltpu.make_async_remote_copy(
            src_ref=b2s.at[piece], dst_ref=b2r.at[piece],
            send_sem=b_send.at[2 + c], recv_sem=b_recv.at[2 + c],
            device_id=(z, x, cross), device_id_type=MESH,
        )

    b1s[0] = acc[far].astype(BF)
    to_mate(0).start()
    b1s[1] = acc[mate].astype(BF)
    to_mate(1).start()
    to_mate(0).wait_recv()
    for c in range(2):
        piece = slice(c * bs, (c + 1) * bs)
        b2s[piece] = (acc[cross, piece] + b1r[0, piece].astype(F32)).astype(BF)
        to_cross(c).start()
    to_mate(1).wait_recv()
    w_copy.wait()
    cot_copy.wait()
    for c in range(2):
        piece = slice(c * bs, (c + 1) * bs)
        known = acc[r, piece] + b1r[1, piece].astype(F32)
        to_cross(c).wait_recv()
        hid[piece] = (known + b2r[piece].astype(F32)).astype(BF)
    hidden = hid[...]
    pre = jnp.dot(hidden, wv[...], preferred_element_type=F32)
    sigmoid_z = 1.0 / (1.0 + jnp.exp(-pre))
    grad_pre = (
        cotv[...].astype(F32) * (sigmoid_z * (1.0 + pre * (1.0 - sigmoid_z)))
    ).astype(BF)
    grad = lax.dot_general(
        hidden, grad_pre, (((0,), (0,)), ((), ())), preferred_element_type=F32
    ).astype(BF)
    stage[...] = grad

    tall = 16
    owners = nx * nrep
    place = x * nrep + r
    owns = (z == 1) | (z == 2)
    quad = owners // 2

    def rank(owner_z, p):
        return p % 2 * owners + (owner_z - 1) * quad + p // 2

    def rows_of(o, n=1):
        return pl.ds(pl.multiple_of(o * tall, tall), n * tall)

    mine = rows_of(rank(jnp.clip(z, 1, 2), place))
    half = rows_of(core * owners, owners)

    def scatter(target_z, p):
        o = target_z * owners + p
        return pltpu.make_async_remote_copy(
            src_ref=stage.at[rows_of(rank(target_z, p))],
            dst_ref=parts.at[(o - me + ndev) % ndev],
            send_sem=d_send.at[0], recv_sem=d_recv.at[0],
            device_id=(target_z, p // nrep, p % nrep), device_id_type=MESH,
        )

    def spray(target_z, q):
        return pltpu.make_async_remote_copy(
            src_ref=gath.at[mine], dst_ref=gath.at[mine],
            send_sem=d_send.at[1], recv_sem=d_recv.at[1],
            device_id=(target_z, q // 2, q % 2 * 2 + core), device_id_type=MESH,
        )

    def chips(target_z, whole):
        for k in range(0 if whole else 1, quad):
            spray(target_z, (place // 2 + k) % quad).start()

    hand_over = pltpu.make_async_remote_copy(
        src_ref=gath.at[half], dst_ref=gath.at[half],
        send_sem=d_send.at[2], recv_sem=d_recv.at[2],
        device_id=(z, x, mate), device_id_type=MESH,
    )

    def plane(send, target_z, whole):
        def one(k, carry):
            send(target_z, (place + k) % owners).start()
            return carry

        lax.fori_loop(0 if whole else 1, owners, one, 0, unroll=True)

    def many(whole, k):
        return pltpu.make_async_remote_copy(
            src_ref=whole, dst_ref=whole,
            send_sem=d_send.at[k], recv_sem=d_recv.at[k],
            device_id=(z, x, mate), device_id_type=MESH,
        )

    @pl.when(z < 2)
    def _():
        plane(scatter, 2, True)

    @pl.when(z >= 2)
    def _():
        plane(scatter, 1, True)

    @pl.when(z == 0)
    def _():
        plane(scatter, 1, True)

    @pl.when(z == nz - 1)
    def _():
        plane(scatter, 2, True)

    @pl.when(owns)
    def _():
        plane(scatter, z, False)

    outv[...] = (pre * sigmoid_z).astype(BF)
    out_copy = pltpu.make_async_copy(outv, out_ref, local_sem.at[3])
    out_copy.start()

    all_parts = parts.at[pl.ds(1, ndev - 1)]
    all_but_one = stage.at[pl.ds(0, (2 * owners - 1) * tall)]

    @pl.when(owns)
    def _():
        total = stage[mine, :].astype(F32)
        many(all_parts, 0).wait_recv()
        for k in range(1, ndev):
            total = total + parts[k].astype(F32)
        gath[mine, :] = total.astype(BF)
        chips(3 * (2 - z), True)
        chips(3 - z, True)
        chips(3 * (z - 1), True)
        chips(z, False)
        many(gath.at[pl.ds(0, (owners - 1) * tall)], 1).wait_recv()

    @pl.when(jnp.logical_not(owns))
    def _():
        many(gath.at[pl.ds(0, owners * tall)], 1).wait_recv()

    hand_over.start()
    for k in range(2):
        to_mate(k).wait_send()
        to_cross(k).wait_send()
    for c in range(pieces):
        late = False
        for src in range(nz):
            @pl.when((z < nz - 1) & (src <= z))
            def _():
                hop(0, src, x, c).wait_send()

            @pl.when((z > 0) & (src >= z))
            def _():
                hop(1, src, x, c).wait_send()

            if late and src in (0, nz - 1):
                @pl.when(z == src)
                def _():
                    hop(2, src, x, c).wait_send()
            else:
                hop(2, src, x, c).wait_send()
        if late:
            @pl.when(z < nz - 1)
            def _():
                hop(0, 0, 1 - x, c).wait_send()

            @pl.when(z > 0)
            def _():
                hop(1, nz - 1, 1 - x, c).wait_send()

    @pl.when(owns)
    def _():
        many(all_but_one, 0).wait_send()
        many(all_but_one, 1).wait_send()

    @pl.when(jnp.logical_not(owns))
    def _():
        many(stage, 0).wait_send()

    hand_over.wait_send()
    hand_over.wait_recv()
    sum_ref[...] = gath[...]
    out_copy.wait()


def finish_kernel(out_in, sum_in, out_ref, wg_ref, outv, sumv, wgv, sems):
    sum_get = pltpu.make_async_copy(sum_in, sumv, sems.at[0])
    out_get = pltpu.make_async_copy(out_in, outv, sems.at[1])
    sum_get.start()
    out_get.start()
    sum_get.wait()
    wgv[...] = sumv[...].astype(F32)
    wg_put = pltpu.make_async_copy(wgv, wg_ref, sems.at[2])
    wg_put.start()
    out_get.wait()
    out_put = pltpu.make_async_copy(outv, out_ref, sems.at[3])
    out_put.start()
    wg_put.wait()
    out_put.wait()


def fused(nz, features, adj_values, adj_cols, adj_count, weight, cotangent):
    rows, _, bs, wide = adj_values.shape
    slots = wide // bs
    width = features.shape[1]
    ndev = nz * 8
    hbm = pl.BlockSpec(memory_space=pl.ANY)
    smem = pl.BlockSpec(memory_space=pltpu.SMEM)
    vmem = pl.BlockSpec(memory_space=pltpu.VMEM)
    own = features.shape[0]
    out, total = pl.pallas_call(
        functools.partial(fused_kernel, nz, rows, slots, bs),
        out_shape=(
            jax.ShapeDtypeStruct(features.shape, BF),
            jax.ShapeDtypeStruct(weight.shape, BF),
        ),
        in_specs=[hbm, hbm, smem, smem, hbm, hbm],
        out_specs=(hbm, vmem),
        scratch_shapes=[
            pltpu.VMEM((nz * 2, own, width), BF),
            pltpu.VMEM((slots, rows, bs, bs), BF),
            pltpu.VMEM((nz * 2, rows * bs, own), BF),
            pltpu.VMEM((4, own, width), F32),
            pltpu.VMEM(weight.shape, BF),
            pltpu.VMEM((own, width), BF),
            pltpu.VMEM((2, own, width), BF),
            pltpu.VMEM((2, own, width), BF),
            pltpu.VMEM((own, width), BF),
            pltpu.VMEM((own, width), BF),
            pltpu.VMEM((own, width), BF),
            pltpu.VMEM((own, width), BF),
            pltpu.VMEM(weight.shape, BF),
            pltpu.VMEM((ndev, 16, width), BF),
            pltpu.VMEM(weight.shape, BF),
            pltpu.SemaphoreType.DMA((4,)),
            pltpu.SemaphoreType.DMA((slots,)),
            pltpu.SemaphoreType.DMA((3, nz * 2, 4)),
            pltpu.SemaphoreType.DMA((nz * 2, 4)),
            pltpu.SemaphoreType.DMA((4,)),
            pltpu.SemaphoreType.DMA((4,)),
            pltpu.SemaphoreType.DMA((3,)),
            pltpu.SemaphoreType.DMA((3,)),
        ],
        compiler_params=pltpu.CompilerParams(collective_id=0, has_side_effects=True),
    )(features, adj_values, adj_cols, adj_count.reshape(-1), weight, cotangent)
    return pl.pallas_call(
        finish_kernel,
        out_shape=(
            jax.ShapeDtypeStruct(out.shape, BF),
            jax.ShapeDtypeStruct(total.shape, F32),
        ),
        in_specs=[hbm, hbm],
        out_specs=(hbm, hbm),
        scratch_shapes=[
            pltpu.VMEM(out.shape, BF),
            pltpu.VMEM(total.shape, BF),
            pltpu.VMEM(total.shape, F32),
            pltpu.SemaphoreType.DMA((4,)),
        ],
    )(out, total)


def solution(mesh):
    placed = (
        P(("cuts", "blk", "rep"), None),
        P(("cuts", "blk"), "rep", None, None),
        P(("cuts", "blk"), "rep", None),
        P(("cuts", "blk"), "rep"),
        P(),
        P(("cuts", "blk", "rep"), None),
    )
    sizes = (mesh.shape["cuts"], mesh.shape["blk"], mesh.shape["rep"])
    body = functools.partial(fused, sizes[0]) if sizes == (4, 2, 4) else local
    return jax.shard_map(
        body,
        mesh=mesh,
        in_specs=placed,
        out_specs=(P(("cuts", "blk", "rep"), None), P()),
        check_vma=False,
    )
```
